768 devices in a mesh: curve: 192 (over y, z, core), slab: 4 (over x).
Axes of the slice: x: 4, y: 8, z: 12, core: 2. Of those that a mesh axis runs over, the one named last changes fastest.
Arguments:
- offset: float32 [3, 768, 16, 128], P(None, 'curve', 'slab'), may hold values from 0 to 1
- velocity: float32 [3, 768, 16, 128], P(None, 'curve', 'slab'), may hold values from -4 to 4
- mass: float32 [768, 16, 128], P('curve', 'slab'), may hold values from 0.00390625 to 0.015625
- smoothing: float32 [768, 16, 128], P('curve', 'slab'), may hold values from 0.35 to 0.5
- energy: float32 [768, 16, 128], P('curve', 'slab'), may hold values from 0.5 to 6
- damage: float32 [768, 16, 128], P('curve', 'slab'), may hold values from 0 to 0.9
- stress: float32 [6, 768, 16, 128], P(None, 'curve', 'slab'), may hold values from -3 to 3
- material: int32 [768, 16, 128], P('curve', 'slab'), may hold values from 0 to 3
- pair_mask: int32 [768, 16, 9], P('curve', 'slab'), may hold values from 0 to 1, as said below
- eos_table: float32 [3, 4], replicated, may hold values from 0.3 to 1.5
Outputs:
- density: float32 [768, 16, 128], P('curve', 'slab')
- kick: float32 [3, 768, 16, 128], P(None, 'curve', 'slab')
- heat: float32 [768, 16, 128], P('curve', 'slab')
- step: float32 [], replicated
The draws below stay inside these ranges and needn't reach their ends.
Inputs may be any that keep to these rules, and one draw needn't show every extreme that they name: `pair_mask`: slot 4, the cell itself, is always 1.
All inputs are finite; a program needn't handle non-finite values.
Results may differ from the reference program's by a relative error of at most 0.0003.
Values sent between devices are 32-bit elements; how exact they have to be, the bound alone decides.
A program may use at most 32 MiB of HBM per device.

```python
import math
import jax
import jax.numpy as jnp
from jax import lax

P_SIZE = 128
NMAT = 4
NCC = 768
NCS = 16


def draw_energy(key, part):
    row_place = jnp.arange(NCC, dtype=jnp.float32)[:, None, None]
    ramp = 1.0 + 2.0 * row_place / max(NCC - 1, 1)
    base = jnp.exp(jax.random.uniform(key, (NCC, NCS, P_SIZE), jnp.float32, math.log(0.5), math.log(2.0)))
    return base * ramp


def draw_pair_mask(key, part):
    picks = jax.random.randint(key, (NCC, NCS, 9), 0, 4)
    kept = (picks > 0).astype(jnp.int32)
    itself = jnp.arange(9, dtype=jnp.int32) == 4
    return jnp.where(itself[None, None, :], 1, kept).astype(jnp.int32)


def plant(drawn, rng, least, high):
    shape = drawn.shape
    place = [jax.random.randint(jax.random.fold_in(rng, axis), (), 0, shape[axis]) for axis in range(len(shape))]
    drawn = drawn.at[tuple(place)].set(least)
    longest = shape.index(max(shape))
    place[longest] = (place[longest] + 1) % shape[longest]
    return drawn.at[tuple(place)].set(high)


def levels(rng, shape, cuts, low, largest):
    level = 1.0
    for dim, parts in cuts:
        steps = jax.random.uniform(jax.random.fold_in(jax.random.fold_in(rng, 6), dim), (parts,), jnp.float32, low / len(cuts), largest / len(cuts))
        level = level * jnp.repeat(jnp.exp(steps), shape[dim] // parts).reshape((-1,) + (1,) * (len(shape) - 1 - dim))
    return level


def normal_values(stream_key, dims, scale, bound, split=(), held_as=jnp.bfloat16):
    entries = jax.random.normal(stream_key, dims, jnp.float32) * scale
    if len(split) > 0:
        entries = levels(stream_key, dims, split, -0.22, 0.18) * entries
    return jnp.clip(entries, min=-bound, max=bound).astype(held_as)


def setup_inputs(seed: int = 0) -> dict:
    keys = jax.random.split(jax.random.key(seed), 11)
    offset = jnp.clip(1.0 * jax.random.uniform(keys[0], (3, NCC, NCS, P_SIZE), jnp.float32) ** levels(keys[0], (3, NCC, NCS, P_SIZE), ((1, 192), (2, 4)), -0.2, 0.2), 0.0, 1.0)
    velocity = normal_values(keys[1], (3, NCC, NCS, P_SIZE), 0.5, 4.0, ((1, 192), (2, 4)), jnp.float32)
    mass = jnp.clip(jnp.exp(math.log(0.015625) - 1.3862944 * jax.random.uniform(keys[2], (NCC, NCS, P_SIZE), jnp.float32) ** levels(keys[2], (NCC, NCS, P_SIZE), ((0, 192), (1, 4)), -0.2, 0.2)), 0.00390625, 0.015625)
    smoothing = jnp.clip(jnp.exp(math.log(0.5) - 0.35667496 * jax.random.uniform(keys[3], (NCC, NCS, P_SIZE), jnp.float32) ** levels(keys[3], (NCC, NCS, P_SIZE), ((0, 192), (1, 4)), -0.2, 0.2)), 0.35, 0.5)
    energy = draw_energy(jax.random.fold_in(keys[10], 71), 0)
    damage = jnp.clip(0.9 * jax.random.uniform(keys[5], (NCC, NCS, P_SIZE), jnp.float32) ** levels(keys[5], (NCC, NCS, P_SIZE), ((0, 192), (1, 4)), -0.2, 0.2), 0.0, 0.9)
    stress = normal_values(keys[6], (6, NCC, NCS, P_SIZE), 0.3, 3.0, ((1, 192), (2, 4)), jnp.float32)
    material = plant(jax.random.randint(keys[7], (NCC, NCS, P_SIZE), 0, NMAT), jax.random.fold_in(keys[7], 1), 0, NMAT - 1).astype(jnp.int32)
    pair_mask = draw_pair_mask(jax.random.fold_in(keys[10], 71), 0)
    eos_table = jnp.clip(jnp.exp(jax.random.uniform(keys[9], (3, NMAT), jnp.float32, math.log(0.3), math.log(1.5))), 0.3, 1.5)
    return {"offset": offset, "velocity": velocity, "mass": mass, "smoothing": smoothing, "energy": energy, "damage": damage, "stress": stress, "material": material, "pair_mask": pair_mask, "eos_table": eos_table}


courant = 0.3
visc_linear = 1.0
visc_square = 2.0
neighbours = [(-1, -1), (-1, 0), (-1, 1), (0, -1), (0, 0), (0, 1), (1, -1), (1, 0), (1, 1)]

def spline_terms(dist_sq, smooth_pair):
    radius = jnp.sqrt(dist_sq)
    dist_ratio = radius / smooth_pair
    norming = 8.0 / (math.pi * smooth_pair ** 3)
    inner_poly = 1.0 - 1.5 * dist_ratio ** 2 + 0.75 * dist_ratio ** 3
    outer_base = jnp.maximum(2.0 - dist_ratio, 0.0)
    outer_poly = 0.25 * outer_base ** 3
    kernel = norming * jnp.where(dist_ratio < 1.0, inner_poly, outer_poly)
    inner_slope = -3.0 + 2.25 * dist_ratio
    outer_slope = -0.75 * outer_base ** 2 / jnp.maximum(dist_ratio, 1.0)
    slope_term = norming / smooth_pair ** 2 * jnp.where(dist_ratio < 1.0, inner_slope, outer_slope)
    return (kernel, slope_term)

def separations(own_cells, partner, step_a, step_b):
    sep_x = own_cells[0][:, :, None] - partner[0][:, None, :] - step_a
    sep_y = own_cells[1][:, :, None] - partner[1][:, None, :] - step_b
    sep_z = own_cells[2][:, :, None] - partner[2][:, None, :]
    smooth_pair = 0.5 * (own_cells[7][:, :, None] + partner[7][:, None, :])
    return (sep_x, sep_y, sep_z, smooth_pair)

def density_rows(kin_pad, pair_mask):
    count_rows = pair_mask.shape[0]
    count_cols = pair_mask.shape[1]

    def one_row(row_index):
        row_block = lax.dynamic_slice_in_dim(kin_pad, row_index, 3, 1)
        pair_flags = lax.dynamic_index_in_dim(pair_mask, row_index, 0, keepdims=False).astype(jnp.float32)
        own_cells = row_block[:, 1, 1:count_cols + 1]
        density_sum = jnp.zeros(own_cells.shape[1:], jnp.float32)
        for slot_index, (step_a, step_b) in enumerate(neighbours):
            partner = row_block[:, 1 + step_a, 1 + step_b:1 + step_b + count_cols]
            sep_x, sep_y, sep_z, smooth_pair = separations(own_cells, partner, step_a, step_b)
            kernel, slope_term = spline_terms(sep_x * sep_x + sep_y * sep_y + sep_z * sep_z, smooth_pair)
            density_sum = density_sum + pair_flags[:, slot_index][:, None] * lax.optimization_barrier(jnp.sum(partner[6][:, None, :] * kernel, axis=2))
        return density_sum
    return lax.map(one_row, jnp.arange(count_rows, dtype=jnp.int32))

def material_state(density, energy, damage, stress, material, eos_table):
    material_hits = material[..., None] == jnp.arange(eos_table.shape[1], dtype=jnp.int32)

    def lookup(values):
        return lax.optimization_barrier(jnp.sum(jnp.where(material_hits, values, 0.0), axis=-1))
    rest_density = lookup(eos_table[0])
    sound_base = lookup(eos_table[1])
    gruneisen = lookup(eos_table[2])
    pressure = sound_base ** 2 * (density - rest_density) + gruneisen * density * energy
    sound_speed = jnp.sqrt(sound_base ** 2 + gruneisen * energy)
    intact = 1.0 - damage
    sigma = jnp.stack([intact * stress[0] - pressure, intact * stress[1] - pressure, intact * stress[2] - pressure, intact * stress[3], intact * stress[4], intact * stress[5]])
    return (sound_speed, sigma / (density * density))

def force_rows(kin_pad, state_pad, pair_mask):
    count_rows = pair_mask.shape[0]
    count_cols = pair_mask.shape[1]

    def one_row(row_index):
        kin_block = lax.dynamic_slice_in_dim(kin_pad, row_index, 3, 1)
        state_block = lax.dynamic_slice_in_dim(state_pad, row_index, 3, 1)
        pair_flags = lax.dynamic_index_in_dim(pair_mask, row_index, 0, keepdims=False).astype(jnp.float32)
        own_kin = kin_block[:, 1, 1:count_cols + 1]
        own_state = state_block[:, 1, 1:count_cols + 1]
        own_q = own_state[2:8][:, :, :, None]
        accel_x = jnp.zeros(own_kin.shape[1:], jnp.float32)
        accel_y = jnp.zeros(own_kin.shape[1:], jnp.float32)
        accel_z = jnp.zeros(own_kin.shape[1:], jnp.float32)
        heating = jnp.zeros(own_kin.shape[1:], jnp.float32)
        for slot_index, (step_a, step_b) in enumerate(neighbours):
            partner_kin = kin_block[:, 1 + step_a, 1 + step_b:1 + step_b + count_cols]
            partner_state = state_block[:, 1 + step_a, 1 + step_b:1 + step_b + count_cols]
            sep_x, sep_y, sep_z, smooth_pair = separations(own_kin, partner_kin, step_a, step_b)
            dist_sq = sep_x * sep_x + sep_y * sep_y + sep_z * sep_z
            kernel, slope_term = spline_terms(dist_sq, smooth_pair)
            grad_x = sep_x * slope_term
            grad_y = sep_y * slope_term
            grad_z = sep_z * slope_term
            rel_vx = own_kin[3][:, :, None] - partner_kin[3][:, None, :]
            rel_vy = own_kin[4][:, :, None] - partner_kin[4][:, None, :]
            rel_vz = own_kin[5][:, :, None] - partner_kin[5][:, None, :]
            pair_mass = partner_kin[6][:, None, :] * pair_flags[:, slot_index][:, None, None]
            sum_q = [own_state[2 + component][:, :, None] + partner_state[2 + component][:, None, :] for component in range(6)]
            push_x = sum_q[0] * grad_x + sum_q[3] * grad_y + sum_q[4] * grad_z
            push_y = sum_q[3] * grad_x + sum_q[1] * grad_y + sum_q[5] * grad_z
            push_z = sum_q[4] * grad_x + sum_q[5] * grad_y + sum_q[2] * grad_z
            work_x = own_q[0] * grad_x + own_q[3] * grad_y + own_q[4] * grad_z
            work_y = own_q[3] * grad_x + own_q[1] * grad_y + own_q[5] * grad_z
            work_z = own_q[4] * grad_x + own_q[5] * grad_y + own_q[2] * grad_z
            approach = rel_vx * sep_x + rel_vy * sep_y + rel_vz * sep_z
            mu_term = smooth_pair * jnp.minimum(approach, 0.0) / (dist_sq + 0.01 * smooth_pair ** 2)
            mean_density = 0.5 * (own_state[0][:, :, None] + partner_state[0][:, None, :])
            mean_sound = 0.5 * (own_state[1][:, :, None] + partner_state[1][:, None, :])
            viscous = (-visc_linear * mean_sound * mu_term + visc_square * mu_term * mu_term) / mean_density
            accel_x = accel_x + lax.optimization_barrier(jnp.sum(pair_mass * (push_x - viscous * grad_x), axis=2))
            accel_y = accel_y + lax.optimization_barrier(jnp.sum(pair_mass * (push_y - viscous * grad_y), axis=2))
            accel_z = accel_z + lax.optimization_barrier(jnp.sum(pair_mass * (push_z - viscous * grad_z), axis=2))
            heat_pair = -(rel_vx * work_x + rel_vy * work_y + rel_vz * work_z) + 0.5 * viscous * (rel_vx * grad_x + rel_vy * grad_y + rel_vz * grad_z)
            heating = heating + lax.optimization_barrier(jnp.sum(pair_mass * heat_pair, axis=2))
        return (jnp.stack([accel_x, accel_y, accel_z]), heating)
    accel, heating = lax.map(one_row, jnp.arange(count_rows, dtype=jnp.int32))
    return (jnp.moveaxis(accel, 0, 1), heating)

def reference(offset, velocity, mass, smoothing, energy, damage, stress, material, pair_mask, eos_table):
    kinematic = jnp.concatenate([offset, velocity, mass[None], smoothing[None]], axis=0)
    kin_pad = jnp.pad(kinematic, ((0, 0), (1, 1), (1, 1), (0, 0)))
    density = density_rows(kin_pad, pair_mask)
    sound_speed, tensor = material_state(density, energy, damage, stress, material, eos_table)
    state = jnp.concatenate([density[None], sound_speed[None], tensor], axis=0)
    state_pad = jnp.pad(state, ((0, 0), (1, 1), (1, 1), (0, 0)))
    accel, heating = force_rows(kin_pad, state_pad, pair_mask)
    speed = jnp.sqrt(lax.optimization_barrier(jnp.sum(velocity * velocity, axis=0)))
    step = jnp.min(courant * smoothing / (sound_speed + speed))
    return (density, step * accel, step * heating, step)
```

```python
import functools
import math

import jax
import jax.numpy as jnp
from jax import lax
from jax.experimental import pallas as pl
from jax.experimental.pallas import tpu as pltpu
from jax.sharding import PartitionSpec as P

F32 = jnp.float32
BF16 = jnp.bfloat16
P_SIZE = 128
COURANT = 0.3
CHUNK = 32
N_IN = 42
N_HALO = 44
DIRS = [(-1, -1), (-1, 0), (-1, 1), (0, -1), (0, 1), (1, -1), (1, 0), (1, 1)]
NT = (((1,), (1,)), ((), ()))


def ge(t, bound):
    return lax.div(t + (64 - bound), 64)


def interior_pair(t):
    s1, s2, s3 = ge(t, 12), ge(t, 24), ge(t, 33)
    u = t - 12 * s1 - 12 * s2 - 9 * s3
    a, b = lax.div(u, 3), lax.rem(u, 3)
    flip = s1 - s2
    row = 1 + a + flip * (b - a)
    col = 1 + b + flip * (a - b) + s3
    return row, col, row + s1, col + 1 - s1 + s2 - 2 * s3


def halo_pair(t):
    s1, s2, s3 = ge(t, 12), ge(t, 24), ge(t, 34)
    u = t - 12 * s1 - 12 * s2 - 10 * s3 + s2
    k = lax.div(u, 3)
    a, b = 1 + k, k + lax.rem(u, 3)
    n2 = 1 - s2
    side = s1 - s2
    row = n2 * (1 + 3 * side) + s2 * a
    col = n2 * a + s2 * (1 + 3 * s3)
    qrow = n2 * 5 * side + s2 * b
    qcol = n2 * b + s2 * 5 * s3
    return row, col, qrow, qcol


def split3(v):
    hi = v.astype(BF16).astype(F32)
    mid = (v - hi).astype(BF16).astype(F32)
    return hi, mid, v - hi - mid


def recip(v):
    r = pl.reciprocal(v, approx=True)
    return r * (2.0 - v * r)


def hilo(v):
    hi = v.astype(BF16)
    return hi, (v - hi.astype(F32)).astype(BF16)


def min_rounds(n_curve, n_slab):
    rounds = []

    def add(axis, stride, size):
        cover = 1
        while cover < size:
            off = min(cover, size - cover)
            rounds.append((axis, stride, size, off))
            cover += off

    if n_curve == 192:
        add(0, 1, 2)
        add(0, 2, 12)
        add(0, 24, 8)
    else:
        add(0, 1, n_curve)
    add(1, 1, n_slab)
    return rounds


def round_peer(spec, curve, slab, sign):
    axis, stride, size, off = spec
    me = curve if axis == 0 else slab
    digit = lax.rem(lax.div(me, stride), size)
    other = lax.rem(digit + size + sign * off, size)
    moved = me + (other - digit) * stride
    return (moved, slab) if axis == 0 else (curve, moved)


def body(
    n_curve,
    n_slab,
    offset,
    velocity,
    mass,
    smoothing,
    energy,
    damage,
    stress,
    material,
    pair_mask,
    eos,
    density_out,
    kick_out,
    heat_out,
    step_out,
    kin,
    state,
    left,
    right,
    left2,
    right2,
    mass_a,
    cols,
    cbf,
    cu,
    geom,
    geom2,
    pair_hi,
    pair_lo,
    w_hi,
    w_lo,
    y_buf,
    mu_buf,
    dacc,
    acc,
    vref,
    msrc,
    mdst,
    kin_send,
    kin_recv,
    st_send,
    st_recv,
    m_send,
    m_recv,
):
    curve = lax.axis_index("curve")
    slab = lax.axis_index("slab")
    rounds = min_rounds(n_curve, n_slab)
    n_rounds = len(rounds)

    def inside(c, s):
        ok = (c >= 0) & (c < n_curve) & (s >= 0) & (s < n_slab)
        return ok

    zero8 = jnp.zeros((8, P_SIZE), F32)
    for buf in (kin, state):
        for c in range(6):
            buf[0, c] = zero8
            buf[5, c] = zero8
        for r in range(1, 5):
            buf[r, 0] = zero8
            buf[r, 5] = zero8

    has_comm = n_curve * n_slab > 1
    if has_comm:
        barrier = pltpu.get_barrier_semaphore()

        def greet(c, s):
            pl.semaphore_signal(
                barrier,
                inc=1,
                device_id={"curve": c, "slab": s},
                device_id_type=pl.DeviceIdType.MESH,
            )

        for dc, ds in DIRS:

            @pl.when(inside(curve + dc, slab + ds))
            def _():
                greet(curve + dc, slab + ds)

        for spec in rounds:
            greet(*round_peer(spec, curve, slab, 1))
            greet(*round_peer(spec, curve, slab, -1))

    def span(d, sending):
        if d == 0:
            return pl.ds(1, 4)
        if sending:
            return pl.ds(4 if d > 0 else 1, 1)
        return pl.ds(0 if d > 0 else 5, 1)

    def halo_copy(buf, send, recv, k):
        dc, ds = DIRS[k]
        return pltpu.make_async_remote_copy(
            src_ref=buf.at[span(dc, True), span(ds, True)],
            dst_ref=buf.at[span(dc, False), span(ds, False)],
            send_sem=send.at[k],
            recv_sem=recv.at[k],
            device_id={"curve": curve + dc, "slab": slab + ds},
            device_id_type=pl.DeviceIdType.MESH,
        )

    def halo_start(buf, send, recv):
        if not has_comm:
            return
        for k, (dc, ds) in enumerate(DIRS):

            @pl.when(inside(curve + dc, slab + ds))
            def _():
                halo_copy(buf, send, recv, k).start()

    def halo_wait(buf, send, recv):
        if not has_comm:
            return
        for k, (dc, ds) in enumerate(DIRS):

            @pl.when(inside(curve - dc, slab - ds))
            def _():
                halo_copy(buf, send, recv, k).wait_recv()

    def halo_drain(buf, send, recv):
        if not has_comm:
            return
        for k, (dc, ds) in enumerate(DIRS):

            @pl.when(inside(curve + dc, slab + ds))
            def _():
                halo_copy(buf, send, recv, k).wait_send()

    def min_copy(r):
        c, s = round_peer(rounds[r], curve, slab, 1)
        return pltpu.make_async_remote_copy(
            src_ref=msrc.at[r],
            dst_ref=mdst.at[r],
            send_sem=m_send.at[r],
            recv_sem=m_recv.at[r],
            device_id={"curve": c, "slab": s},
            device_id_type=pl.DeviceIdType.MESH,
        )

    def min_fold(r):
        min_copy(r).wait_recv()
        msrc[r + 1] = jnp.minimum(msrc[r], mdst[r])

    for r in range(4):
        for c in range(3):
            kin[r + 1, 1:5, c, :] = offset[c, r]
            kin[r + 1, 1:5, 3 + c, :] = velocity[c, r]
        kin[r + 1, 1:5, 6, :] = mass[r]
        kin[r + 1, 1:5, 7, :] = smoothing[r]

    bound = jnp.full((4, P_SIZE), jnp.inf, F32)
    for r in range(4):
        mat = material[r]
        base = jnp.zeros((4, P_SIZE), F32)
        grun = jnp.zeros((4, P_SIZE), F32)
        for n in range(4):
            base = base + jnp.where(mat == n, eos[1, n], 0.0)
            grun = grun + jnp.where(mat == n, eos[2, n], 0.0)
        sound = jnp.sqrt(base * base + grun * energy[r])
        state[r + 1, 1:5, 1, :] = sound
        vx, vy, vz = velocity[0, r], velocity[1, r], velocity[2, r]
        speed = jnp.sqrt(vx * vx + vy * vy + vz * vz)
        bound = jnp.minimum(bound, COURANT * smoothing[r] / (sound + speed))
    msrc[0] = jnp.broadcast_to(jnp.min(bound, axis=0, keepdims=True), (8, P_SIZE))

    total = zero8
    for r in range(1, 5):
        for c in range(1, 5):
            total = total + kin[r, c]
    mean = jnp.sum(total, axis=1, keepdims=True) * (1.0 / (16 * P_SIZE))
    row_id = lax.broadcasted_iota(jnp.int32, (8, P_SIZE), 0)
    is_v = (row_id >= 3) & (row_id < 6)
    vref[...] = jnp.where(is_v, jnp.broadcast_to(mean, (8, P_SIZE)), 0.0)
    eye = (
        lax.broadcasted_iota(jnp.int32, (P_SIZE, P_SIZE), 0)
        == lax.broadcasted_iota(jnp.int32, (P_SIZE, P_SIZE), 1)
    ).astype(BF16)

    is_x = row_id < 3
    is_h = row_id == 7

    def shifted(r, c):
        add = jnp.where(
            row_id == 0,
            r.astype(F32) - 3.0,
            jnp.where(row_id == 1, c.astype(F32) - 3.0, jnp.where(row_id == 2, -0.5, 0.0)),
        )
        return kin[r, c] + add - vref[...]

    def stack_rows(rows):
        out = jnp.zeros((8, P_SIZE), F32)
        for i, v in enumerate(rows):
            if isinstance(v, float):
                v = jnp.full((8, P_SIZE), v, F32)
            else:
                v = jnp.broadcast_to(v, (8, P_SIZE))
            out = jnp.where(row_id == i, v, out)
        return out

    def prepare(r, c):
        cell = r * 6 + c
        v = shifted(r, c)
        m = v[6:7]
        x = [v[i : i + 1] for i in range(3)]
        u = [v[i : i + 1] for i in range(3, 6)]
        n2 = x[0] * x[0] + x[1] * x[1] + x[2] * x[2]
        vx = x[0] * u[0] + x[1] * u[1] + x[2] * u[2]
        n2s, vxs = split3(n2), split3(vx)
        vs = split3(v)
        h, md, lo = vs
        g6 = stack_rows([*n2s, *vxs, 1.0, 1.0])
        g7 = stack_rows([1.0])
        lt = jnp.concatenate([h, h, h, md, md, lo, g6, g7], axis=0).astype(BF16)
        left[cell] = lax.dot_general(eye, lt, NT, preferred_element_type=F32).astype(BF16)
        pick = (0, 1, 2, 0, 1, 0)
        wa = [jnp.where(is_x, -2.0 * s, 0.0) for s in vs]
        wb = [
            jnp.where(is_x, -4.0 * pltpu.roll(s, 5, 0), jnp.where(is_v, -4.0 * pltpu.roll(s, 3, 0), 0.0))
            for s in vs
        ]
        half_h = jnp.where(is_h, 0.5, 0.0)
        hs = [0.5 * s[7:8] for s in vs]
        ra = [wa[i] for i in pick] + [
            stack_rows([1.0, 1.0, 1.0, 0.0, 0.0, 0.0, n2s[0], n2s[1]]),
            stack_rows([n2s[2]]),
        ]
        rb = [wb[i] for i in pick] + [
            stack_rows([0.0, 0.0, 0.0, 4.0, 4.0, 4.0, 4.0 * vxs[0], 4.0 * vxs[1]]),
            stack_rows([4.0 * vxs[2]]),
        ]
        rc = [half_h, zero8, zero8, half_h, zero8, half_h] + [
            stack_rows([0.0, 0.0, 0.0, 0.0, 0.0, 0.0, hs[0], hs[1]]),
            stack_rows([hs[2]]),
        ]
        for i, part in enumerate((ra, rb, rc)):
            right[cell, :, i * P_SIZE : (i + 1) * P_SIZE] = jnp.concatenate(part, axis=0).astype(BF16)
        ms = m * (2.0 / math.pi)
        mh = ms.astype(BF16).astype(F32)
        ml = ms - mh
        mass_a[cell, 0:16] = jnp.concatenate([stack_rows([mh, ml]), zero8], axis=0).astype(BF16)
        mass_a[cell, 16:32] = jnp.concatenate([stack_rows([mh]), zero8], axis=0).astype(BF16)
        mc = m * (-6.0 / math.pi)
        g0 = jnp.where(row_id == 6, 1.0, jnp.where(is_h, 0.0, v)) * mc
        g1 = stack_rows(
            [
                x[0] * u[0],
                x[1] * u[1],
                x[2] * u[2],
                x[0] * u[1] + x[1] * u[0],
                x[0] * u[2] + x[2] * u[0],
                x[1] * u[2] + x[2] * u[1],
            ]
        ) * mc
        g01 = jnp.concatenate([g0, g1], axis=0)
        a, b = hilo(g01)
        cbf[cell, 0:16] = a
        cbf[cell, 32:48] = b
        cu[cell, 0:16] = a
        cu[cell, 16:32] = b

    def prepare2(r, c):
        cell = r * 6 + c
        v = shifted(r, c)
        s = state[r, c]
        x = [v[i : i + 1] for i in range(3)]
        mc = v[6:7] * (-6.0 / math.pi)
        ss = split3(s)
        lt = jnp.concatenate([*ss, stack_rows([1.0, 1.0, 1.0])], axis=0).astype(BF16)
        left2[cell] = lax.dot_general(eye, lt, NT, preferred_element_type=F32).astype(BF16)
        for i in range(2):
            one = jnp.where(row_id == i, 1.0, 0.0)
            part = [one, one, one, stack_rows([w[i : i + 1] for w in ss])]
            right2[cell, :, i * P_SIZE : (i + 1) * P_SIZE] = jnp.concatenate(part, axis=0).astype(BF16)
        txx, tyy, tzz, txy, txz, tyz = [s[i : i + 1] for i in range(2, 8)]
        g2 = jnp.where(row_id < 6, pltpu.roll(s, 6, 0), 0.0) * mc
        g3 = stack_rows(
            [
                txx * x[0] + txy * x[1] + txz * x[2],
                txy * x[0] + tyy * x[1] + tyz * x[2],
                txz * x[0] + tyz * x[1] + tzz * x[2],
            ]
        ) * mc
        a, b = hilo(jnp.concatenate([g2, g3], axis=0))
        cbf[cell, 16:32] = a
        cbf[cell, 48:64] = b

    def own_cells(fn):
        def run(n, carry):
            fn(1 + lax.div(n, 4), 1 + lax.rem(n, 4))
            return carry

        lax.fori_loop(0, 16, run, 0)

    def halo_cells(fn):
        def run(n, carry):
            s1, s2 = ge(n, 6), ge(n, 12)
            u = n - 12
            row = (1 - s2) * 5 * s1 + s2 * (1 + lax.div(u + 16, 2) - 8)
            col = (1 - s2) * (n - 6 * s1) + s2 * 5 * lax.rem(u + 16, 2)
            fn(row, col)
            return carry

        lax.fori_loop(0, 20, run, 0)

    def flag(r, c, k):
        return pair_mask[r - 1, c - 1, k].astype(F32)

    def tile_one(pr, pc, qr, qc, t, both):
        p, q = pr * 6 + pc, qr * 6 + qc
        geom[...] = jnp.dot(left[q], right[p], preferred_element_type=F32)
        for s in range(P_SIZE // CHUNK):
            rows = slice(s * CHUNK, (s + 1) * CHUNK)
            r2 = jnp.maximum(geom[rows, 0:128], 1e-12)
            close = jnp.minimum(geom[rows, 128:256], 0.0)
            inv = recip(geom[rows, 256:384])
            inv2 = inv * inv
            t2 = r2 * inv2
            rinv = lax.rsqrt(t2)
            ratio = t2 * rinv
            near = ratio < 1.0
            q3 = 3.0 * ratio
            base = jnp.maximum(2.0 - ratio, 0.0)
            base2 = base * base
            poly = jnp.where(near, 4.0 + t2 * (q3 - 6.0), base2 * base)
            slope = jnp.where(near, 4.0 - q3, base2 * rinv)
            inv3 = inv2 * inv
            a, b = hilo(inv3 * poly)
            pair_hi[rows] = a
            pair_lo[rows] = b
            w = (inv3 * inv2) * slope
            a, b = hilo(w)
            w_hi[t, rows] = a
            w_lo[t, rows] = b
            mu = (inv * close) * recip(t2 + 0.01)
            mu_buf[t, rows] = mu
            y_buf[t, rows] = w * mu
        own_p = (pr - 1) * 4 + pc - 1
        kp = 3 * (qr - pr + 1) + qc - pc + 1
        sums = jnp.dot(mass_a[q, 0:16], pair_hi[...], preferred_element_type=F32) + jnp.dot(
            mass_a[q, 16:32], pair_lo[...], preferred_element_type=F32
        )
        dacc[own_p] += flag(pr, pc, kp) * sums
        if both:
            own_q = (qr - 1) * 4 + qc - 1
            sums = lax.dot_general(
                mass_a[p, 0:16], pair_hi[...], NT, preferred_element_type=F32
            ) + lax.dot_general(mass_a[p, 16:32], pair_lo[...], NT, preferred_element_type=F32)
            dacc[own_q] += flag(qr, qc, 8 - kp) * sums

    def tile_two(pr, pc, qr, qc, t, both):
        p, q = pr * 6 + pc, qr * 6 + qc
        geom2[...] = jnp.dot(left2[q], right2[p], preferred_element_type=F32)
        for s in range(P_SIZE // CHUNK):
            rows = slice(s * CHUNK, (s + 1) * CHUNK)
            u = y_buf[t, rows] * (mu_buf[t, rows] - geom2[rows, 128:256]) * recip(geom2[rows, 0:128])
            a, b = hilo(u)
            pair_hi[rows] = a
            pair_lo[rows] = b

        def fold(owner, src, flagged, dims):
            def mul(a, b):
                return lax.dot_general(a, b, dims, preferred_element_type=F32)

            full = mul(cbf[src], w_hi[t])
            sums = full[0:32] + full[32:64] + mul(cbf[src, 0:32], w_lo[t])
            acc[owner, 0:32] += flagged * sums
            full = mul(cu[src], pair_hi[...])
            sums = full[0:16] + full[16:32] + mul(cu[src, 0:16], pair_lo[...])
            acc[owner, 32:48] += flagged * sums

        kp = 3 * (qr - pr + 1) + qc - pc + 1
        fold((pr - 1) * 4 + pc - 1, q, flag(pr, pc, kp), (((1,), (0,)), ((), ())))
        if both:
            fold((qr - 1) * 4 + qc - 1, p, flag(qr, qc, 8 - kp), NT)

    def self_loop(tile, hook=None):
        def run(n, carry):
            r, c = 1 + lax.div(n, 4), 1 + lax.rem(n, 4)
            if hook:
                hook(n)
            tile(r, c, r, c, n, False)
            return carry

        lax.fori_loop(0, 16, run, 0)

    def interior_loop(tile, hook=None):
        def run(n, carry):
            if hook:
                hook(n)
            tile(*interior_pair(n), 16 + n, True)
            return carry

        lax.fori_loop(0, N_IN, run, 0)

    def halo_loop(tile, hook=None):
        def run(n, carry):
            if hook:
                hook(n)
            tile(*halo_pair(n), 16 + N_IN + n, False)
            return carry

        lax.fori_loop(0, N_HALO, run, 0)

    def make_hook(events):
        if not has_comm or not events:
            return None

        def hook(n):
            for when, fns in events.items():

                @pl.when(n == when)
                def _():
                    for fn in fns:
                        fn()

        return hook

    slots = [("a", 2), ("a", 14), ("a", 26), ("a", 38), ("b", 8), ("b", 22), ("b", 36), ("c", 3), ("d", 8), ("d", 24), ("d", 40)]
    events = {"a": {}, "b": {}, "c": {}, "d": {}}
    for r in range(n_rounds + 1):
        loop, when = slots[r]
        if r > 0:
            events[loop].setdefault(when, []).append(functools.partial(min_fold, r - 1))
        if r < n_rounds:
            events[loop].setdefault(when + 1, []).append(lambda r=r: min_copy(r).start())

    def clear(n, carry):
        dacc[n] = jnp.zeros((16, P_SIZE), F32)
        acc[n] = jnp.zeros((48, P_SIZE), F32)
        return carry

    lax.fori_loop(0, 16, clear, 0)

    if has_comm:
        expected = 2 * n_rounds
        for dc, ds in DIRS:
            expected = expected + inside(curve + dc, slab + ds).astype(jnp.int32)
        pl.semaphore_wait(barrier, expected)
    halo_start(kin, kin_send, kin_recv)

    own_cells(prepare)
    self_loop(tile_one)
    interior_loop(tile_one, make_hook(events["a"]))
    halo_wait(kin, kin_send, kin_recv)
    halo_cells(prepare)
    halo_loop(tile_one, make_hook(events["b"]))

    for r in range(4):
        dens = dacc[4 * r : 4 * r + 4, 0, :] + dacc[4 * r : 4 * r + 4, 1, :]
        density_out[r] = dens
        mat = material[r]
        rest = jnp.zeros((4, P_SIZE), F32)
        base = jnp.zeros((4, P_SIZE), F32)
        grun = jnp.zeros((4, P_SIZE), F32)
        for n in range(4):
            rest = rest + jnp.where(mat == n, eos[0, n], 0.0)
            base = base + jnp.where(mat == n, eos[1, n], 0.0)
            grun = grun + jnp.where(mat == n, eos[2, n], 0.0)
        pressure = base * base * (dens - rest) + grun * dens * energy[r]
        intact = 1.0 - damage[r]
        over = 1.0 / (dens * dens)
        state[r + 1, 1:5, 0, :] = dens
        for k in range(6):
            sigma = intact * stress[k, r]
            if k < 3:
                sigma = sigma - pressure
            state[r + 1, 1:5, 2 + k, :] = sigma * over

    own_cells(prepare2)
    halo_start(state, st_send, st_recv)
    self_loop(tile_two, make_hook(events["c"]))
    interior_loop(tile_two, make_hook(events["d"]))
    halo_wait(state, st_send, st_recv)
    halo_cells(prepare2)
    halo_loop(tile_two)

    if has_comm:
        halo_drain(kin, kin_send, kin_recv)
        halo_drain(state, st_send, st_recv)
        for r in range(n_rounds):
            min_copy(r).wait_send()
    step = jnp.min(msrc[n_rounds if has_comm else 0], axis=(0, 1), keepdims=True)
    step_out[...] = jnp.broadcast_to(step, (8, P_SIZE))

    vm = vref[...]
    for r in range(4):
        cells = slice(4 * r, 4 * r + 4)
        col_id = lax.broadcasted_iota(jnp.int32, (4, P_SIZE), 0).astype(F32)
        x = [offset[0, r] + (r + 1 - 3.0), offset[1, r] + (col_id + (1.0 - 3.0)), offset[2, r] - 0.5]
        u = [velocity[k, r] - vm[3 + k : 4 + k] for k in range(3)]
        txx, tyy, tzz, txy, txz, tyz = [state[r + 1, 1:5, 2 + k, :] for k in range(6)]
        sx = [acc[cells, k, :] for k in range(3)]
        sv = [acc[cells, 3 + k, :] for k in range(3)]
        s1 = acc[cells, 6, :]
        svx = [acc[cells, 8 + k, :] for k in range(6)]
        ax = [acc[cells, 16 + k, :] for k in range(6)]
        bx = [acc[cells, 24 + k, :] for k in range(3)]
        ux = [acc[cells, 32 + k, :] for k in range(3)]
        uv = [acc[cells, 35 + k, :] for k in range(3)]
        u1 = acc[cells, 38, :]
        uvx = acc[cells, 40, :] + acc[cells, 41, :] + acc[cells, 42, :]
        g = [x[k] * s1 - sx[k] for k in range(3)]
        push = [
            txx * g[0] + txy * g[1] + txz * g[2] + (ax[0] * x[0] + ax[3] * x[1] + ax[4] * x[2] - bx[0]),
            txy * g[0] + tyy * g[1] + tyz * g[2] + (ax[3] * x[0] + ax[1] * x[1] + ax[5] * x[2] - bx[1]),
            txz * g[0] + tyz * g[1] + tzz * g[2] + (ax[4] * x[0] + ax[5] * x[1] + ax[2] * x[2] - bx[2]),
        ]
        for k in range(3):
            drag = 0.25 * (x[k] * u1 - ux[k])
            kick_out[k, r] = step * (push[k] - drag)

        def moment(i, j):
            return u[i] * g[j] - x[j] * sv[i]

        mxx = moment(0, 0) + svx[0]
        myy = moment(1, 1) + svx[1]
        mzz = moment(2, 2) + svx[2]
        mxy = moment(0, 1) + moment(1, 0) + svx[3]
        mxz = moment(0, 2) + moment(2, 0) + svx[4]
        myz = moment(1, 2) + moment(2, 1) + svx[5]
        work = txx * mxx + tyy * myy + tzz * mzz + txy * mxy + txz * mxz + tyz * myz
        visc = uvx
        for k in range(3):
            visc = visc + u[k] * (x[k] * u1 - ux[k]) - x[k] * uv[k]
        heat_out[r] = step * (0.125 * visc - work)


def on_device(n_curve, n_slab, *args):
    vmem = pl.BlockSpec(memory_space=pltpu.VMEM)
    smem = pl.BlockSpec(memory_space=pltpu.SMEM)
    n_rounds = max(len(min_rounds(n_curve, n_slab)), 1)
    tiles = 16 + N_IN + N_HALO
    square = (P_SIZE, P_SIZE)
    comm = n_curve * n_slab > 1
    params = dict(vmem_limit_bytes=56 * 1024 * 1024)
    if comm:
        params.update(collective_id=0, has_side_effects=True)
    density, kick, heat, step = pl.pallas_call(
        functools.partial(body, n_curve, n_slab),
        out_shape=(
            jax.ShapeDtypeStruct((4, 4, P_SIZE), F32),
            jax.ShapeDtypeStruct((3, 4, 4, P_SIZE), F32),
            jax.ShapeDtypeStruct((4, 4, P_SIZE), F32),
            jax.ShapeDtypeStruct((8, P_SIZE), F32),
        ),
        in_specs=[vmem] * 8 + [smem, smem],
        out_specs=(vmem, vmem, vmem, vmem),
        scratch_shapes=[
            pltpu.VMEM((6, 6, 8, P_SIZE), F32),
            pltpu.VMEM((6, 6, 8, P_SIZE), F32),
            pltpu.VMEM((36, P_SIZE, 64), BF16),
            pltpu.VMEM((36, 64, 3 * P_SIZE), BF16),
            pltpu.VMEM((36, P_SIZE, 32), BF16),
            pltpu.VMEM((36, 32, 2 * P_SIZE), BF16),
            pltpu.VMEM((36, 32, P_SIZE), BF16),
            pltpu.VMEM((8, P_SIZE), F32),
            pltpu.VMEM((36, 64, P_SIZE), BF16),
            pltpu.VMEM((36, 32, P_SIZE), BF16),
            pltpu.VMEM((P_SIZE, 3 * P_SIZE), F32),
            pltpu.VMEM((P_SIZE, 2 * P_SIZE), F32),
            pltpu.VMEM(square, BF16),
            pltpu.VMEM(square, BF16),
            pltpu.VMEM((tiles, *square), BF16),
            pltpu.VMEM((tiles, *square), BF16),
            pltpu.VMEM((tiles, *square), F32),
            pltpu.VMEM((tiles, *square), F32),
            pltpu.VMEM((16, 16, P_SIZE), F32),
            pltpu.VMEM((16, 48, P_SIZE), F32),
            pltpu.VMEM((8, P_SIZE), F32),
            pltpu.VMEM((n_rounds + 1, 8, P_SIZE), F32),
            pltpu.VMEM((n_rounds, 8, P_SIZE), F32),
            pltpu.SemaphoreType.DMA((8,)),
            pltpu.SemaphoreType.DMA((8,)),
            pltpu.SemaphoreType.DMA((8,)),
            pltpu.SemaphoreType.DMA((8,)),
            pltpu.SemaphoreType.DMA((n_rounds,)),
            pltpu.SemaphoreType.DMA((n_rounds,)),
        ],
        compiler_params=pltpu.CompilerParams(**params),
    )(*args)
    return density, kick, heat, step[0, 0]


def solution(mesh):
    in_specs = (
        P(None, "curve", "slab", None),
        P(None, "curve", "slab", None),
        P("curve", "slab", None),
        P("curve", "slab", None),
        P("curve", "slab", None),
        P("curve", "slab", None),
        P(None, "curve", "slab", None),
        P("curve", "slab", None),
        P("curve", "slab", None),
        P(),
    )
    out_specs = (
        P("curve", "slab", None),
        P(None, "curve", "slab", None),
        P("curve", "slab", None),
        P(),
    )
    run = functools.partial(on_device, mesh.shape["curve"], mesh.shape["slab"])
    return jax.shard_map(run, mesh=mesh, in_specs=in_specs, out_specs=out_specs, check_vma=False)
```

```python
import functools
import math

import jax
import jax.numpy as jnp
from jax import lax
from jax.experimental import pallas as pl
from jax.experimental.pallas import tpu as pltpu
from jax.sharding import PartitionSpec as P

F32 = jnp.float32
BF16 = jnp.bfloat16
P_SIZE = 128
COURANT = 0.3
CHUNK = 32
N_IN = 42
N_HALO = 44
DIRS = [(-1, -1), (-1, 0), (-1, 1), (0, -1), (0, 1), (1, -1), (1, 0), (1, 1)]
NT = (((1,), (1,)), ((), ()))


def ge(t, bound):
    return lax.div(t + (64 - bound), 64)


def interior_pair(t):
    s1, s2, s3 = ge(t, 12), ge(t, 24), ge(t, 33)
    u = t - 12 * s1 - 12 * s2 - 9 * s3
    a, b = lax.div(u, 3), lax.rem(u, 3)
    flip = s1 - s2
    row = 1 + a + flip * (b - a)
    col = 1 + b + flip * (a - b) + s3
    return row, col, row + s1, col + 1 - s1 + s2 - 2 * s3


def halo_pair(t):
    s1, s2, s3 = ge(t, 12), ge(t, 24), ge(t, 34)
    u = t - 12 * s1 - 12 * s2 - 10 * s3 + s2
    k = lax.div(u, 3)
    a, b = 1 + k, k + lax.rem(u, 3)
    n2 = 1 - s2
    side = s1 - s2
    row = n2 * (1 + 3 * side) + s2 * a
    col = n2 * a + s2 * (1 + 3 * s3)
    qrow = n2 * 5 * side + s2 * b
    qcol = n2 * b + s2 * 5 * s3
    return row, col, qrow, qcol


def split3(v):
    hi = v.astype(BF16).astype(F32)
    mid = (v - hi).astype(BF16).astype(F32)
    return hi, mid, v - hi - mid


def recip(v):
    return 1.0 / v


def to_float(n):
    return float(n) if isinstance(n, int) else n.astype(F32)


def hilo(v):
    hi = v.astype(BF16)
    return hi, (v - hi.astype(F32)).astype(BF16)


def min_rounds(n_curve, n_slab):
    if n_curve % 24:
        return [[(0, 1, n_curve)], [(1, 1, n_slab)]]
    return [[(0, 2, 12)], [(0, 24, n_curve // 24)], [(0, 1, 2), (1, 1, n_slab)]]


def group_peers(group, curve, slab):
    peers = [(curve, slab)]
    for axis, stride, size in group:
        grown = []
        for c, s in peers:
            me = c if axis == 0 else s
            digit = lax.rem(lax.div(me, stride), size)
            for off in range(size):
                moved = me + (lax.rem(digit + off, size) - digit) * stride
                grown.append((moved, s) if axis == 0 else (c, moved))
        peers = grown
    return peers[1:]


def group_sizes(n_curve, n_slab):
    sizes = []
    for group in min_rounds(n_curve, n_slab):
        size = 1
        for part in group:
            size *= part[2]
        sizes.append(size - 1)
    return sizes


def body(
    n_curve,
    n_slab,
    offset,
    velocity,
    mass,
    smoothing,
    energy,
    damage,
    stress,
    material,
    pair_mask,
    eos,
    density_out,
    kick_out,
    heat_out,
    step_out,
    kin,
    state,
    left,
    right,
    left2,
    right2,
    mass_a,
    cols,
    cbf,
    cu,
    geom,
    pair_hi,
    pair_lo,
    w_hi,
    w_lo,
    y_buf,
    mu_buf,
    dacc,
    acc,
    vref,
    msrc,
    mdst,
    kin_send,
    kin_recv,
    st_send,
    st_recv,
    m_send,
    m_recv,
):
    curve = lax.axis_index("curve")
    slab = lax.axis_index("slab")
    groups = min_rounds(n_curve, n_slab)
    sizes = group_sizes(n_curve, n_slab)

    def inside(c, s):
        ok = (c >= 0) & (c < n_curve) & (s >= 0) & (s < n_slab)
        return ok

    zero8 = jnp.zeros((8, P_SIZE), F32)
    for buf in (kin, state):
        for c in range(6):
            buf[0, c] = zero8
            buf[5, c] = zero8
        for r in range(1, 5):
            buf[r, 0] = zero8
            buf[r, 5] = zero8

    has_comm = n_curve * n_slab > 1
    if has_comm:
        barrier = pltpu.get_barrier_semaphore()

        def greet(c, s):
            pl.semaphore_signal(
                barrier,
                inc=1,
                device_id={"curve": c, "slab": s},
                device_id_type=pl.DeviceIdType.MESH,
            )

        for dc, ds in DIRS:

            @pl.when(inside(curve + dc, slab + ds))
            def _():
                greet(curve + dc, slab + ds)

        for group in groups:
            for peer in group_peers(group, curve, slab):
                greet(*peer)

    def span(d, sending):
        if d == 0:
            return pl.ds(1, 4)
        if sending:
            return pl.ds(4 if d > 0 else 1, 1)
        return pl.ds(0 if d > 0 else 5, 1)

    def halo_copy(buf, send, recv, k):
        dc, ds = DIRS[k]
        return pltpu.make_async_remote_copy(
            src_ref=buf.at[span(dc, True), span(ds, True)],
            dst_ref=buf.at[span(dc, False), span(ds, False)],
            send_sem=send.at[k],
            recv_sem=recv.at[k],
            device_id={"curve": curve + dc, "slab": slab + ds},
            device_id_type=pl.DeviceIdType.MESH,
        )

    def halo_start(buf, send, recv):
        if not has_comm:
            return
        for k, (dc, ds) in enumerate(DIRS):

            @pl.when(inside(curve + dc, slab + ds))
            def _():
                halo_copy(buf, send, recv, k).start()

    def halo_wait(buf, send, recv):
        if not has_comm:
            return
        for k, (dc, ds) in enumerate(DIRS):

            @pl.when(inside(curve - dc, slab - ds))
            def _():
                halo_copy(buf, send, recv, k).wait_recv()

    def halo_drain(buf, send, recv):
        if not has_comm:
            return
        for k, (dc, ds) in enumerate(DIRS):

            @pl.when(inside(curve + dc, slab + ds))
            def _():
                halo_copy(buf, send, recv, k).wait_send()

    def min_copies(r):
        first = sum(sizes[:r])
        return [
            pltpu.make_async_remote_copy(
                src_ref=msrc.at[r],
                dst_ref=mdst.at[first + k],
                send_sem=m_send.at[first + k],
                recv_sem=m_recv.at[first + k],
                device_id={"curve": c, "slab": s},
                device_id_type=pl.DeviceIdType.MESH,
            )
            for k, (c, s) in enumerate(group_peers(groups[r], curve, slab))
        ]

    def min_start(r):
        if has_comm:
            for copy in min_copies(r):
                copy.start()

    def min_fold(r):
        if has_comm:
            low = msrc[r]
            for k, copy in enumerate(min_copies(r)):
                copy.wait_recv()
                low = jnp.minimum(low, mdst[sum(sizes[:r]) + k])
            msrc[r + 1] = low

    for r in range(4):
        for c in range(3):
            kin[r + 1, 1:5, c, :] = offset[c, r]
            kin[r + 1, 1:5, 3 + c, :] = velocity[c, r]
        kin[r + 1, 1:5, 6, :] = mass[r]
        kin[r + 1, 1:5, 7, :] = smoothing[r]

    bound = jnp.full((4, P_SIZE), jnp.inf, F32)
    for r in range(4):
        mat = material[r]
        base = jnp.zeros((4, P_SIZE), F32)
        grun = jnp.zeros((4, P_SIZE), F32)
        for n in range(4):
            base = base + jnp.where(mat == n, eos[1, n], 0.0)
            grun = grun + jnp.where(mat == n, eos[2, n], 0.0)
        sound = jnp.sqrt(base * base + grun * energy[r])
        state[r + 1, 1:5, 1, :] = sound
        vx, vy, vz = velocity[0, r], velocity[1, r], velocity[2, r]
        speed = jnp.sqrt(vx * vx + vy * vy + vz * vz)
        bound = jnp.minimum(bound, COURANT * smoothing[r] / (sound + speed))
    msrc[0] = jnp.broadcast_to(jnp.min(bound, axis=0, keepdims=True), (8, P_SIZE))

    total = zero8
    for r in range(1, 5):
        for c in range(1, 5):
            total = total + kin[r, c]
    mean = jnp.sum(total, axis=1, keepdims=True) * (1.0 / (16 * P_SIZE))
    row_id = lax.broadcasted_iota(jnp.int32, (8, P_SIZE), 0)
    is_v = (row_id >= 3) & (row_id < 6)
    vref[...] = jnp.where(is_v, jnp.broadcast_to(mean, (8, P_SIZE)), 0.0)
    eye = (
        lax.broadcasted_iota(jnp.int32, (P_SIZE, P_SIZE), 0)
        == lax.broadcasted_iota(jnp.int32, (P_SIZE, P_SIZE), 1)
    ).astype(BF16)

    is_x = row_id < 3
    is_h = row_id == 7

    def shifted(r, c):
        add = jnp.where(
            row_id == 0,
            to_float(r) - 3.0,
            jnp.where(row_id == 1, to_float(c) - 3.0, jnp.where(row_id == 2, -0.5, 0.0)),
        )
        return kin[r, c] + add - vref[...]

    def stack_rows(rows):
        out = jnp.zeros((8, P_SIZE), F32)
        for i, v in enumerate(rows):
            if isinstance(v, float):
                v = jnp.full((8, P_SIZE), v, F32)
            else:
                v = jnp.broadcast_to(v, (8, P_SIZE))
            out = jnp.where(row_id == i, v, out)
        return out

    def prepare(r, c):
        cell = r * 6 + c
        v = shifted(r, c)
        m = v[6:7]
        x = [v[i : i + 1] for i in range(3)]
        u = [v[i : i + 1] for i in range(3, 6)]
        n2 = x[0] * x[0] + x[1] * x[1] + x[2] * x[2]
        vx = x[0] * u[0] + x[1] * u[1] + x[2] * u[2]
        n2s, vxs = split3(n2), split3(vx)
        vs = split3(v)
        h, md, lo = vs
        g6 = stack_rows([*n2s, *vxs, 1.0, 1.0])
        g7 = stack_rows([1.0])
        lt = jnp.concatenate([h, h, h, md, md, lo, g6, g7], axis=0).astype(BF16)
        left[cell] = lax.dot_general(eye, lt, NT, preferred_element_type=F32).astype(BF16)
        pick = (0, 1, 2, 0, 1, 0)
        wa = [jnp.where(is_x, -2.0 * s, 0.0) for s in vs]
        wb = [
            jnp.where(is_x, -4.0 * pltpu.roll(s, 5, 0), jnp.where(is_v, -4.0 * pltpu.roll(s, 3, 0), 0.0))
            for s in vs
        ]
        half_h = jnp.where(is_h, 0.5, 0.0)
        hs = [0.5 * s[7:8] for s in vs]
        ra = [wa[i] for i in pick] + [
            stack_rows([1.0, 1.0, 1.0, 0.0, 0.0, 0.0, n2s[0], n2s[1]]),
            stack_rows([n2s[2]]),
        ]
        rb = [wb[i] for i in pick] + [
            stack_rows([0.0, 0.0, 0.0, 4.0, 4.0, 4.0, 4.0 * vxs[0], 4.0 * vxs[1]]),
            stack_rows([4.0 * vxs[2]]),
        ]
        rc = [half_h, zero8, zero8, half_h, zero8, half_h] + [
            stack_rows([0.0, 0.0, 0.0, 0.0, 0.0, 0.0, hs[0], hs[1]]),
            stack_rows([hs[2]]),
        ]
        for i, part in enumerate((ra, rb, rc)):
            right[cell, :, i * P_SIZE : (i + 1) * P_SIZE] = jnp.concatenate(part, axis=0).astype(BF16)
        ms = m * (2.0 / math.pi)
        mh = ms.astype(BF16).astype(F32)
        ml = ms - mh
        mass_a[cell, 0:16] = jnp.concatenate([stack_rows([mh, ml]), zero8], axis=0).astype(BF16)
        mass_a[cell, 16:32] = jnp.concatenate([stack_rows([mh]), zero8], axis=0).astype(BF16)
        mc = m * (-6.0 / math.pi)
        g0 = jnp.where(row_id == 6, 1.0, jnp.where(is_h, 0.0, v)) * mc
        g1 = stack_rows(
            [
                x[0] * u[0],
                x[1] * u[1],
                x[2] * u[2],
                x[0] * u[1] + x[1] * u[0],
                x[0] * u[2] + x[2] * u[0],
                x[1] * u[2] + x[2] * u[1],
            ]
        ) * mc
        g01 = jnp.concatenate([g0, g1], axis=0)
        a, b = hilo(g01)
        cbf[cell, 0:16] = a
        cbf[cell, 32:48] = b
        cu[cell, 0:16] = a
        cu[cell, 16:32] = b

    def prepare2(r, c):
        cell = r * 6 + c
        v = shifted(r, c)
        s = state[r, c]
        x = [v[i : i + 1] for i in range(3)]
        mc = v[6:7] * (-6.0 / math.pi)
        ss = split3(s)
        lt = jnp.concatenate([*ss, stack_rows([1.0, 1.0, 1.0])], axis=0).astype(BF16)
        left2[cell] = lax.dot_general(eye, lt, NT, preferred_element_type=F32).astype(BF16)
        for i in range(2):
            one = jnp.where(row_id == i, 1.0, 0.0)
            part = [one, one, one, stack_rows([w[i : i + 1] for w in ss])]
            right2[cell, :, i * P_SIZE : (i + 1) * P_SIZE] = jnp.concatenate(part, axis=0).astype(BF16)
        txx, tyy, tzz, txy, txz, tyz = [s[i : i + 1] for i in range(2, 8)]
        g2 = jnp.where(row_id < 6, pltpu.roll(s, 6, 0), 0.0) * mc
        g3 = stack_rows(
            [
                txx * x[0] + txy * x[1] + txz * x[2],
                txy * x[0] + tyy * x[1] + tyz * x[2],
                txz * x[0] + tyz * x[1] + tzz * x[2],
            ]
        ) * mc
        a, b = hilo(jnp.concatenate([g2, g3], axis=0))
        cbf[cell, 16:32] = a
        cbf[cell, 48:64] = b

    def own_cells(fn):
        def run(n, carry):
            for k in range(4):
                fn(1 + n, 1 + k)
            return carry

        lax.fori_loop(0, 4, run, 0)

    def halo_cells(fn):
        def run(n, carry):
            for k in range(4):
                m = 4 * n + k
                s1, s2 = ge(m, 6), ge(m, 12)
                u = m + 4
                row = (1 - s2) * 5 * s1 + s2 * (lax.div(u, 2) - 7)
                col = (1 - s2) * (m - 6 * s1) + s2 * 5 * lax.rem(u, 2)
                fn(row, col)
            return carry

        lax.fori_loop(0, 5, run, 0)

    def flag(r, c, k):
        return pair_mask[r - 1, c - 1, k].astype(F32)

    def tiles_one(group, both):
        for i, (pr, pc, qr, qc, t) in enumerate(group):
            geom[i][...] = jnp.dot(left[qr * 6 + qc], right[pr * 6 + pc], preferred_element_type=F32)
        for i, (pr, pc, qr, qc, t) in enumerate(group):
            for s in range(P_SIZE // CHUNK):
                rows = slice(s * CHUNK, (s + 1) * CHUNK)
                r2 = jnp.maximum(geom[i][rows, 0:128], 1e-12)
                close = jnp.minimum(geom[i][rows, 128:256], 0.0)
                inv = recip(geom[i][rows, 256:384])
                inv2 = inv * inv
                t2 = r2 * inv2
                rinv = lax.rsqrt(t2)
                ratio = t2 * rinv
                near = ratio < 1.0
                q3 = 3.0 * ratio
                base = jnp.maximum(2.0 - ratio, 0.0)
                base2 = base * base
                poly = jnp.where(near, 4.0 + t2 * (q3 - 6.0), base2 * base)
                slope = jnp.where(near, 4.0 - q3, base2 * rinv)
                inv3 = inv2 * inv
                a, b = hilo(inv3 * poly)
                pair_hi[i][rows] = a
                pair_lo[i][rows] = b
                w = (inv3 * inv2) * slope
                a, b = hilo(w)
                w_hi[t, rows] = a
                w_lo[t, rows] = b
                mu = (inv * close) * recip(t2 + 0.01)
                mu_buf[t, rows] = mu
                y_buf[t, rows] = w * mu
        for i, (pr, pc, qr, qc, t) in enumerate(group):
            p, q = pr * 6 + pc, qr * 6 + qc
            own_p = (pr - 1) * 4 + pc - 1
            kp = 3 * (qr - pr + 1) + qc - pc + 1
            sums = jnp.dot(mass_a[q, 0:16], pair_hi[i][...], preferred_element_type=F32) + jnp.dot(
                mass_a[q, 16:32], pair_lo[i][...], preferred_element_type=F32
            )
            dacc[own_p] += flag(pr, pc, kp) * sums
            if both:
                own_q = (qr - 1) * 4 + qc - 1
                sums = lax.dot_general(
                    mass_a[p, 0:16], pair_hi[i][...], NT, preferred_element_type=F32
                ) + lax.dot_general(mass_a[p, 16:32], pair_lo[i][...], NT, preferred_element_type=F32)
                dacc[own_q] += flag(qr, qc, 8 - kp) * sums

    def tiles_two(group, both):
        for i, (pr, pc, qr, qc, t) in enumerate(group):
            geom[i][:, 0:256] = jnp.dot(left2[qr * 6 + qc], right2[pr * 6 + pc], preferred_element_type=F32)
        for i, (pr, pc, qr, qc, t) in enumerate(group):
            for s in range(P_SIZE // CHUNK):
                rows = slice(s * CHUNK, (s + 1) * CHUNK)
                u = (
                    y_buf[t, rows]
                    * (mu_buf[t, rows] - geom[i][rows, 128:256])
                    * recip(geom[i][rows, 0:128])
                )
                a, b = hilo(u)
                pair_hi[i][rows] = a
                pair_lo[i][rows] = b

        def fold(i, t, owner, src, flagged, dims):
            def mul(a, b):
                return lax.dot_general(a, b, dims, preferred_element_type=F32)

            full = mul(cbf[src], w_hi[t])
            sums = full[0:32] + full[32:64] + mul(cbf[src, 0:32], w_lo[t])
            acc[owner, 0:32] += flagged * sums
            full = mul(cu[src], pair_hi[i][...])
            sums = full[0:16] + full[16:32] + mul(cu[src, 0:16], pair_lo[i][...])
            acc[owner, 32:48] += flagged * sums

        for i, (pr, pc, qr, qc, t) in enumerate(group):
            p, q = pr * 6 + pc, qr * 6 + qc
            kp = 3 * (qr - pr + 1) + qc - pc + 1
            fold(i, t, (pr - 1) * 4 + pc - 1, q, flag(pr, pc, kp), (((1,), (0,)), ((), ())))
            if both:
                fold(i, t, (qr - 1) * 4 + qc - 1, p, flag(qr, qc, 8 - kp), NT)

    def self_tile(n):
        r, c = 1 + lax.div(n, 4), 1 + lax.rem(n, 4)
        return r, c, r, c, n

    def interior_tile(n):
        return (*interior_pair(n), 16 + n)

    def halo_tile(n):
        return (*halo_pair(n), 16 + N_IN + n)

    def tile_loop(tiles, pick, both, count, width):
        def one(n, carry):
            tiles([pick(n * width + k) for k in range(width)], both)
            return carry

        lax.fori_loop(0, count // width, one, 0)

    def clear(n, carry):
        dacc[n] = jnp.zeros((16, P_SIZE), F32)
        acc[n] = jnp.zeros((48, P_SIZE), F32)
        return carry

    lax.fori_loop(0, 16, clear, 0)

    own_cells(prepare)
    tile_loop(tiles_one, self_tile, False, 16, 4)
    if has_comm:
        expected = sum(sizes)
        for dc, ds in DIRS:
            expected = expected + inside(curve + dc, slab + ds).astype(jnp.int32)
        pl.semaphore_wait(barrier, expected)
    halo_start(kin, kin_send, kin_recv)
    min_start(0)
    tile_loop(tiles_one, interior_tile, True, N_IN, 3)
    halo_wait(kin, kin_send, kin_recv)
    min_fold(0)
    halo_cells(prepare)
    min_start(1)
    tile_loop(tiles_one, halo_tile, False, N_HALO, 4)

    for r in range(4):
        dens = dacc[4 * r : 4 * r + 4, 0, :] + dacc[4 * r : 4 * r + 4, 1, :]
        density_out[r] = dens
        mat = material[r]
        rest = jnp.zeros((4, P_SIZE), F32)
        base = jnp.zeros((4, P_SIZE), F32)
        grun = jnp.zeros((4, P_SIZE), F32)
        for n in range(4):
            rest = rest + jnp.where(mat == n, eos[0, n], 0.0)
            base = base + jnp.where(mat == n, eos[1, n], 0.0)
            grun = grun + jnp.where(mat == n, eos[2, n], 0.0)
        pressure = base * base * (dens - rest) + grun * dens * energy[r]
        intact = 1.0 - damage[r]
        over = 1.0 / (dens * dens)
        state[r + 1, 1:5, 0, :] = dens
        for k in range(6):
            sigma = intact * stress[k, r]
            if k < 3:
                sigma = sigma - pressure
            state[r + 1, 1:5, 2 + k, :] = sigma * over

    own_cells(prepare2)
    halo_start(state, st_send, st_recv)
    tile_loop(tiles_two, self_tile, False, 16, 4)
    min_fold(1)
    tile_loop(tiles_two, interior_tile, True, N_IN, 3)
    halo_wait(state, st_send, st_recv)
    if len(groups) > 2:
        min_start(2)
    halo_cells(prepare2)
    tile_loop(tiles_two, halo_tile, False, N_HALO, 4)
    if len(groups) > 2:
        min_fold(2)

    if has_comm:
        halo_drain(kin, kin_send, kin_recv)
        halo_drain(state, st_send, st_recv)
        for r in range(len(groups)):
            for copy in min_copies(r):
                copy.wait_send()
    step = jnp.min(msrc[len(groups) if has_comm else 0], axis=(0, 1), keepdims=True)
    step_out[...] = jnp.broadcast_to(step, (8, P_SIZE))

    vm = vref[...]
    for r in range(4):
        cells = slice(4 * r, 4 * r + 4)
        col_id = lax.broadcasted_iota(jnp.int32, (4, P_SIZE), 0).astype(F32)
        x = [offset[0, r] + (r + 1 - 3.0), offset[1, r] + (col_id + (1.0 - 3.0)), offset[2, r] - 0.5]
        u = [velocity[k, r] - vm[3 + k : 4 + k] for k in range(3)]
        txx, tyy, tzz, txy, txz, tyz = [state[r + 1, 1:5, 2 + k, :] for k in range(6)]
        sx = [acc[cells, k, :] for k in range(3)]
        sv = [acc[cells, 3 + k, :] for k in range(3)]
        s1 = acc[cells, 6, :]
        svx = [acc[cells, 8 + k, :] for k in range(6)]
        ax = [acc[cells, 16 + k, :] for k in range(6)]
        bx = [acc[cells, 24 + k, :] for k in range(3)]
        ux = [acc[cells, 32 + k, :] for k in range(3)]
        uv = [acc[cells, 35 + k, :] for k in range(3)]
        u1 = acc[cells, 38, :]
        uvx = acc[cells, 40, :] + acc[cells, 41, :] + acc[cells, 42, :]
        g = [x[k] * s1 - sx[k] for k in range(3)]
        push = [
            txx * g[0] + txy * g[1] + txz * g[2] + (ax[0] * x[0] + ax[3] * x[1] + ax[4] * x[2] - bx[0]),
            txy * g[0] + tyy * g[1] + tyz * g[2] + (ax[3] * x[0] + ax[1] * x[1] + ax[5] * x[2] - bx[1]),
            txz * g[0] + tyz * g[1] + tzz * g[2] + (ax[4] * x[0] + ax[5] * x[1] + ax[2] * x[2] - bx[2]),
        ]
        for k in range(3):
            drag = 0.25 * (x[k] * u1 - ux[k])
            kick_out[k, r] = step * (push[k] - drag)

        def moment(i, j):
            return u[i] * g[j] - x[j] * sv[i]

        mxx = moment(0, 0) + svx[0]
        myy = moment(1, 1) + svx[1]
        mzz = moment(2, 2) + svx[2]
        mxy = moment(0, 1) + moment(1, 0) + svx[3]
        mxz = moment(0, 2) + moment(2, 0) + svx[4]
        myz = moment(1, 2) + moment(2, 1) + svx[5]
        work = txx * mxx + tyy * myy + tzz * mzz + txy * mxy + txz * mxz + tyz * myz
        visc = uvx
        for k in range(3):
            visc = visc + u[k] * (x[k] * u1 - ux[k]) - x[k] * uv[k]
        heat_out[r] = step * (0.125 * visc - work)


def on_device(n_curve, n_slab, *args):
    vmem = pl.BlockSpec(memory_space=pltpu.VMEM)
    smem = pl.BlockSpec(memory_space=pltpu.SMEM)
    n_rounds = len(min_rounds(n_curve, n_slab))
    n_peers = max(sum(group_sizes(n_curve, n_slab)), 1)
    tiles = 16 + N_IN + N_HALO
    square = (P_SIZE, P_SIZE)
    comm = n_curve * n_slab > 1
    params = dict(vmem_limit_bytes=56 * 1024 * 1024)
    if comm:
        params.update(collective_id=0, has_side_effects=True)
    density, kick, heat, step = pl.pallas_call(
        functools.partial(body, n_curve, n_slab),
        out_shape=(
            jax.ShapeDtypeStruct((4, 4, P_SIZE), F32),
            jax.ShapeDtypeStruct((3, 4, 4, P_SIZE), F32),
            jax.ShapeDtypeStruct((4, 4, P_SIZE), F32),
            jax.ShapeDtypeStruct((8, P_SIZE), F32),
        ),
        in_specs=[vmem] * 8 + [smem, smem],
        out_specs=(vmem, vmem, vmem, vmem),
        scratch_shapes=[
            pltpu.VMEM((6, 6, 8, P_SIZE), F32),
            pltpu.VMEM((6, 6, 8, P_SIZE), F32),
            pltpu.VMEM((36, P_SIZE, 64), BF16),
            pltpu.VMEM((36, 64, 3 * P_SIZE), BF16),
            pltpu.VMEM((36, P_SIZE, 32), BF16),
            pltpu.VMEM((36, 32, 2 * P_SIZE), BF16),
            pltpu.VMEM((36, 32, P_SIZE), BF16),
            pltpu.VMEM((8, P_SIZE), F32),
            pltpu.VMEM((36, 64, P_SIZE), BF16),
            pltpu.VMEM((36, 32, P_SIZE), BF16),
            [pltpu.VMEM((P_SIZE, 3 * P_SIZE), F32) for _ in range(4)],
            [pltpu.VMEM(square, BF16) for _ in range(4)],
            [pltpu.VMEM(square, BF16) for _ in range(4)],
            pltpu.VMEM((tiles, *square), BF16),
            pltpu.VMEM((tiles, *square), BF16),
            pltpu.VMEM((tiles, *square), F32),
            pltpu.VMEM((tiles, *square), F32),
            pltpu.VMEM((16, 16, P_SIZE), F32),
            pltpu.VMEM((16, 48, P_SIZE), F32),
            pltpu.VMEM((8, P_SIZE), F32),
            pltpu.VMEM((n_rounds + 1, 8, P_SIZE), F32),
            pltpu.VMEM((n_peers, 8, P_SIZE), F32),
            pltpu.SemaphoreType.DMA((8,)),
            pltpu.SemaphoreType.DMA((8,)),
            pltpu.SemaphoreType.DMA((8,)),
            pltpu.SemaphoreType.DMA((8,)),
            pltpu.SemaphoreType.DMA((n_peers,)),
            pltpu.SemaphoreType.DMA((n_peers,)),
        ],
        compiler_params=pltpu.CompilerParams(**params),
    )(*args)
    return density, kick, heat, step[0, 0]


def solution(mesh):
    in_specs = (
        P(None, "curve", "slab", None),
        P(None, "curve", "slab", None),
        P("curve", "slab", None),
        P("curve", "slab", None),
        P("curve", "slab", None),
        P("curve", "slab", None),
        P(None, "curve", "slab", None),
        P("curve", "slab", None),
        P("curve", "slab", None),
        P(),
    )
    out_specs = (
        P("curve", "slab", None),
        P(None, "curve", "slab", None),
        P("curve", "slab", None),
        P(),
    )
    run = functools.partial(on_device, mesh.shape["curve"], mesh.shape["slab"])
    return jax.shard_map(run, mesh=mesh, in_specs=in_specs, out_specs=out_specs, check_vma=False)
```

```python
import functools
import math

import jax
import jax.numpy as jnp
from jax import lax
from jax.experimental import pallas as pl
from jax.experimental.pallas import tpu as pltpu
from jax.sharding import PartitionSpec as P

F32 = jnp.float32
BF16 = jnp.bfloat16
P_SIZE = 128
COURANT = 0.3
CHUNK = 32
TILES = 16 + 42 + 44
WIDEST = 10
DIRS = [(-1, -1), (-1, 0), (-1, 1), (0, -1), (0, 1), (1, -1), (1, 0), (1, 1)]
NT = (((1,), (1,)), ((), ()))


def split3(v):
    hi = v.astype(BF16).astype(F32)
    mid = (v - hi).astype(BF16).astype(F32)
    return hi, mid, v - hi - mid


def recip(v):
    return 1.0 / v


def to_float(n):
    return float(n) if isinstance(n, int) else n.astype(F32)


def hilo(v):
    hi = v.astype(BF16)
    return hi, (v - hi.astype(F32)).astype(BF16)


def min_rounds(n_curve, n_slab):
    if n_curve % 24:
        return [[(0, 1, n_curve)], [(1, 1, n_slab)]]
    return [[(0, 2, 12)], [(0, 24, n_curve // 24)], [(0, 1, 2), (1, 1, n_slab)]]


def group_peers(group, curve, slab):
    peers = [(curve, slab)]
    for axis, stride, size in group:
        grown = []
        for c, s in peers:
            me = c if axis == 0 else s
            digit = lax.rem(lax.div(me, stride), size)
            for off in range(size):
                moved = me + (lax.rem(digit + off, size) - digit) * stride
                grown.append((moved, s) if axis == 0 else (c, moved))
        peers = grown
    return peers[1:]


def group_sizes(n_curve, n_slab):
    sizes = []
    for group in min_rounds(n_curve, n_slab):
        size = 1
        for part in group:
            size *= part[2]
        sizes.append(size - 1)
    return sizes


def body(
    n_curve,
    n_slab,
    offset,
    velocity,
    mass,
    smoothing,
    energy,
    damage,
    stress,
    material,
    pair_mask,
    eos,
    density_out,
    kick_out,
    heat_out,
    step_out,
    kin,
    state,
    left,
    right,
    left2,
    right2,
    mass_a,
    cols,
    cbf,
    cu,
    geom,
    pair_hi,
    pair_lo,
    w_hi,
    w_lo,
    y_buf,
    mu_buf,
    dacc,
    acc,
    vref,
    msrc,
    mdst,
    kin_send,
    kin_recv,
    st_send,
    st_recv,
    m_send,
    m_recv,
):
    curve = lax.axis_index("curve")
    slab = lax.axis_index("slab")
    groups = min_rounds(n_curve, n_slab)
    sizes = group_sizes(n_curve, n_slab)

    def inside(c, s):
        ok = (c >= 0) & (c < n_curve) & (s >= 0) & (s < n_slab)
        return ok

    zero8 = jnp.zeros((8, P_SIZE), F32)
    for buf in (kin, state):
        for c in range(6):
            buf[0, c] = zero8
            buf[5, c] = zero8
        for r in range(1, 5):
            buf[r, 0] = zero8
            buf[r, 5] = zero8

    has_comm = n_curve * n_slab > 1
    if has_comm:
        barrier = pltpu.get_barrier_semaphore()

        def greet(c, s):
            pl.semaphore_signal(
                barrier,
                inc=1,
                device_id={"curve": c, "slab": s},
                device_id_type=pl.DeviceIdType.MESH,
            )

        for dc, ds in DIRS:

            @pl.when(inside(curve + dc, slab + ds))
            def _():
                greet(curve + dc, slab + ds)

        for group in groups:
            for peer in group_peers(group, curve, slab):
                greet(*peer)

    def span(d, sending):
        if d == 0:
            return pl.ds(1, 4)
        if sending:
            return pl.ds(4 if d > 0 else 1, 1)
        return pl.ds(0 if d > 0 else 5, 1)

    def halo_copy(buf, send, recv, k):
        dc, ds = DIRS[k]
        return pltpu.make_async_remote_copy(
            src_ref=buf.at[span(dc, True), span(ds, True)],
            dst_ref=buf.at[span(dc, False), span(ds, False)],
            send_sem=send.at[k],
            recv_sem=recv.at[k],
            device_id={"curve": curve + dc, "slab": slab + ds},
            device_id_type=pl.DeviceIdType.MESH,
        )

    def halo_start(buf, send, recv):
        if not has_comm:
            return
        for k, (dc, ds) in enumerate(DIRS):

            @pl.when(inside(curve + dc, slab + ds))
            def _():
                halo_copy(buf, send, recv, k).start()

    def halo_wait(buf, send, recv):
        if not has_comm:
            return
        for k, (dc, ds) in enumerate(DIRS):

            @pl.when(inside(curve - dc, slab - ds))
            def _():
                halo_copy(buf, send, recv, k).wait_recv()

    def halo_drain(buf, send, recv):
        if not has_comm:
            return
        for k, (dc, ds) in enumerate(DIRS):

            @pl.when(inside(curve + dc, slab + ds))
            def _():
                halo_copy(buf, send, recv, k).wait_send()

    def min_copies(r):
        first = sum(sizes[:r])
        return [
            pltpu.make_async_remote_copy(
                src_ref=msrc.at[r],
                dst_ref=mdst.at[first + k],
                send_sem=m_send.at[first + k],
                recv_sem=m_recv.at[first + k],
                device_id={"curve": c, "slab": s},
                device_id_type=pl.DeviceIdType.MESH,
            )
            for k, (c, s) in enumerate(group_peers(groups[r], curve, slab))
        ]

    def min_start(r):
        if has_comm:
            for copy in min_copies(r):
                copy.start()

    def min_fold(r):
        if has_comm:
            low = msrc[r]
            for k, copy in enumerate(min_copies(r)):
                copy.wait_recv()
                low = jnp.minimum(low, mdst[sum(sizes[:r]) + k])
            msrc[r + 1] = low

    for r in range(4):
        for c in range(3):
            kin[r + 1, 1:5, c, :] = offset[c, r]
            kin[r + 1, 1:5, 3 + c, :] = velocity[c, r]
        kin[r + 1, 1:5, 6, :] = mass[r]
        kin[r + 1, 1:5, 7, :] = smoothing[r]

    bound = jnp.full((4, P_SIZE), jnp.inf, F32)
    for r in range(4):
        mat = material[r]
        base = jnp.zeros((4, P_SIZE), F32)
        grun = jnp.zeros((4, P_SIZE), F32)
        for n in range(4):
            base = base + jnp.where(mat == n, eos[1, n], 0.0)
            grun = grun + jnp.where(mat == n, eos[2, n], 0.0)
        sound = jnp.sqrt(base * base + grun * energy[r])
        state[r + 1, 1:5, 1, :] = sound
        vx, vy, vz = velocity[0, r], velocity[1, r], velocity[2, r]
        speed = jnp.sqrt(vx * vx + vy * vy + vz * vz)
        bound = jnp.minimum(bound, COURANT * smoothing[r] / (sound + speed))
    msrc[0] = jnp.broadcast_to(jnp.min(bound, axis=0, keepdims=True), (8, P_SIZE))

    total = zero8
    for r in range(1, 5):
        for c in range(1, 5):
            total = total + kin[r, c]
    mean = jnp.sum(total, axis=1, keepdims=True) * (1.0 / (16 * P_SIZE))
    row_id = lax.broadcasted_iota(jnp.int32, (8, P_SIZE), 0)
    is_v = (row_id >= 3) & (row_id < 6)
    vref[...] = jnp.where(is_v, jnp.broadcast_to(mean, (8, P_SIZE)), 0.0)
    eye = (
        lax.broadcasted_iota(jnp.int32, (P_SIZE, P_SIZE), 0)
        == lax.broadcasted_iota(jnp.int32, (P_SIZE, P_SIZE), 1)
    ).astype(BF16)

    is_x = row_id < 3
    is_h = row_id == 7

    def shifted(r, c):
        add = jnp.where(
            row_id == 0,
            to_float(r) - 3.0,
            jnp.where(row_id == 1, to_float(c) - 3.0, jnp.where(row_id == 2, -0.5, 0.0)),
        )
        return kin[r, c] + add - vref[...]

    def stack_rows(rows):
        out = jnp.zeros((8, P_SIZE), F32)
        for i, v in enumerate(rows):
            if isinstance(v, float):
                v = jnp.full((8, P_SIZE), v, F32)
            else:
                v = jnp.broadcast_to(v, (8, P_SIZE))
            out = jnp.where(row_id == i, v, out)
        return out

    def prepare(r, c):
        cell = r * 6 + c
        v = shifted(r, c)
        m = v[6:7]
        x = [v[i : i + 1] for i in range(3)]
        u = [v[i : i + 1] for i in range(3, 6)]
        n2 = x[0] * x[0] + x[1] * x[1] + x[2] * x[2]
        vx = x[0] * u[0] + x[1] * u[1] + x[2] * u[2]
        n2s, vxs = split3(n2), split3(vx)
        vs = split3(v)
        h, md, lo = vs
        g6 = stack_rows([*n2s, *vxs, 1.0, 1.0])
        g7 = stack_rows([1.0])
        lt = jnp.concatenate([h, h, h, md, md, lo, g6, g7], axis=0).astype(BF16)
        left[cell] = lax.dot_general(eye, lt, NT, preferred_element_type=F32).astype(BF16)
        pick = (0, 1, 2, 0, 1, 0)
        wa = [jnp.where(is_x, -2.0 * s, 0.0) for s in vs]
        wb = [
            jnp.where(is_x, -4.0 * pltpu.roll(s, 5, 0), jnp.where(is_v, -4.0 * pltpu.roll(s, 3, 0), 0.0))
            for s in vs
        ]
        half_h = jnp.where(is_h, 0.5, 0.0)
        hs = [0.5 * s[7:8] for s in vs]
        ra = [wa[i] for i in pick] + [
            stack_rows([1.0, 1.0, 1.0, 0.0, 0.0, 0.0, n2s[0], n2s[1]]),
            stack_rows([n2s[2]]),
        ]
        rb = [wb[i] for i in pick] + [
            stack_rows([0.0, 0.0, 0.0, 4.0, 4.0, 4.0, 4.0 * vxs[0], 4.0 * vxs[1]]),
            stack_rows([4.0 * vxs[2]]),
        ]
        rc = [half_h, zero8, zero8, half_h, zero8, half_h] + [
            stack_rows([0.0, 0.0, 0.0, 0.0, 0.0, 0.0, hs[0], hs[1]]),
            stack_rows([hs[2]]),
        ]
        for i, part in enumerate((ra, rb, rc)):
            right[cell, :, i * P_SIZE : (i + 1) * P_SIZE] = jnp.concatenate(part, axis=0).astype(BF16)
        ms = m * (2.0 / math.pi)
        mh = ms.astype(BF16).astype(F32)
        ml = ms - mh
        mass_a[cell, 0:16] = jnp.concatenate([stack_rows([mh, ml]), zero8], axis=0).astype(BF16)
        mass_a[cell, 16:32] = jnp.concatenate([stack_rows([mh]), zero8], axis=0).astype(BF16)
        mc = m * (-6.0 / math.pi)
        g0 = jnp.where(row_id == 6, 1.0, jnp.where(is_h, 0.0, v)) * mc
        g1 = stack_rows(
            [
                x[0] * u[0],
                x[1] * u[1],
                x[2] * u[2],
                x[0] * u[1] + x[1] * u[0],
                x[0] * u[2] + x[2] * u[0],
                x[1] * u[2] + x[2] * u[1],
            ]
        ) * mc
        g01 = jnp.concatenate([g0, g1], axis=0)
        a, b = hilo(g01)
        cbf[cell, 0:16] = a
        cbf[cell, 32:48] = b
        cu[cell, 0:16] = a
        cu[cell, 16:32] = b

    def prepare2(r, c):
        cell = r * 6 + c
        v = shifted(r, c)
        s = state[r, c]
        x = [v[i : i + 1] for i in range(3)]
        mc = v[6:7] * (-6.0 / math.pi)
        ss = split3(s)
        lt = jnp.concatenate([*ss, stack_rows([1.0, 1.0, 1.0])], axis=0).astype(BF16)
        left2[cell] = lax.dot_general(eye, lt, NT, preferred_element_type=F32).astype(BF16)
        for i in range(2):
            one = jnp.where(row_id == i, 1.0, 0.0)
            part = [one, one, one, stack_rows([w[i : i + 1] for w in ss])]
            right2[cell, :, i * P_SIZE : (i + 1) * P_SIZE] = jnp.concatenate(part, axis=0).astype(BF16)
        txx, tyy, tzz, txy, txz, tyz = [s[i : i + 1] for i in range(2, 8)]
        g2 = jnp.where(row_id < 6, pltpu.roll(s, 6, 0), 0.0) * mc
        g3 = stack_rows(
            [
                txx * x[0] + txy * x[1] + txz * x[2],
                txy * x[0] + tyy * x[1] + tyz * x[2],
                txz * x[0] + tyz * x[1] + tzz * x[2],
            ]
        ) * mc
        a, b = hilo(jnp.concatenate([g2, g3], axis=0))
        cbf[cell, 16:32] = a
        cbf[cell, 48:64] = b

    def own_cells(fn):
        def run(n, carry):
            for k in range(4):
                fn(1 + n, 1 + k)
            return carry

        lax.fori_loop(0, 4, run, 0)

    def halo_cells(fn):
        def outer_rows(n, carry):
            for c in range(6):
                fn(5 * n, c)
            return carry

        def outer_cols(n, carry):
            for r in range(1, 5):
                fn(r, 5 * n)
            return carry

        lax.fori_loop(0, 2, outer_rows, 0)
        lax.fori_loop(0, 2, outer_cols, 0)

    def flag(r, c, k):
        return pair_mask[r - 1, c - 1, k].astype(F32)

    def tiles_one(group, both):
        for i, (pr, pc, qr, qc, t) in enumerate(group):
            geom[i][...] = jnp.dot(left[qr * 6 + qc], right[pr * 6 + pc], preferred_element_type=F32)
        for i, (pr, pc, qr, qc, t) in enumerate(group):
            for s in range(P_SIZE // CHUNK):
                rows = slice(s * CHUNK, (s + 1) * CHUNK)
                r2 = jnp.maximum(geom[i][rows, 0:128], 1e-12)
                close = jnp.minimum(geom[i][rows, 128:256], 0.0)
                inv = recip(geom[i][rows, 256:384])
                inv2 = inv * inv
                t2 = r2 * inv2
                rinv = lax.rsqrt(t2)
                ratio = t2 * rinv
                near = ratio < 1.0
                q3 = 3.0 * ratio
                base = jnp.maximum(2.0 - ratio, 0.0)
                base2 = base * base
                poly = jnp.where(near, 4.0 + t2 * (q3 - 6.0), base2 * base)
                slope = jnp.where(near, 4.0 - q3, base2 * rinv)
                inv3 = inv2 * inv
                a, b = hilo(inv3 * poly)
                pair_hi[i][rows] = a
                pair_lo[i][rows] = b
                w = (inv3 * inv2) * slope
                a, b = hilo(w)
                w_hi[t, rows] = a
                w_lo[t, rows] = b
                mu = (inv * close) * recip(t2 + 0.01)
                mu_buf[t, rows] = mu
                y_buf[t, rows] = w * mu
        for i, (pr, pc, qr, qc, t) in enumerate(group):
            p, q = pr * 6 + pc, qr * 6 + qc
            own_p = (pr - 1) * 4 + pc - 1
            kp = 3 * (qr - pr + 1) + qc - pc + 1
            sums = jnp.dot(mass_a[q, 0:16], pair_hi[i][...], preferred_element_type=F32) + jnp.dot(
                mass_a[q, 16:32], pair_lo[i][...], preferred_element_type=F32
            )
            dacc[own_p] += flag(pr, pc, kp) * sums
            if both:
                own_q = (qr - 1) * 4 + qc - 1
                sums = lax.dot_general(
                    mass_a[p, 0:16], pair_hi[i][...], NT, preferred_element_type=F32
                ) + lax.dot_general(mass_a[p, 16:32], pair_lo[i][...], NT, preferred_element_type=F32)
                dacc[own_q] += flag(qr, qc, 8 - kp) * sums

    def tiles_two(group, both):
        for i, (pr, pc, qr, qc, t) in enumerate(group):
            geom[i][:, 0:256] = jnp.dot(left2[qr * 6 + qc], right2[pr * 6 + pc], preferred_element_type=F32)
        for i, (pr, pc, qr, qc, t) in enumerate(group):
            for s in range(P_SIZE // CHUNK):
                rows = slice(s * CHUNK, (s + 1) * CHUNK)
                u = (
                    y_buf[t, rows]
                    * (mu_buf[t, rows] - geom[i][rows, 128:256])
                    * recip(geom[i][rows, 0:128])
                )
                a, b = hilo(u)
                pair_hi[i][rows] = a
                pair_lo[i][rows] = b

        def fold(i, t, owner, src, flagged, dims):
            def mul(a, b):
                return lax.dot_general(a, b, dims, preferred_element_type=F32)

            full = mul(cbf[src], w_hi[t])
            sums = full[0:32] + full[32:64] + mul(cbf[src, 0:32], w_lo[t])
            acc[owner, 0:32] += flagged * sums
            full = mul(cu[src], pair_hi[i][...])
            sums = full[0:16] + full[16:32] + mul(cu[src, 0:16], pair_lo[i][...])
            acc[owner, 32:48] += flagged * sums

        for i, (pr, pc, qr, qc, t) in enumerate(group):
            p, q = pr * 6 + pc, qr * 6 + qc
            kp = 3 * (qr - pr + 1) + qc - pc + 1
            fold(i, t, (pr - 1) * 4 + pc - 1, q, flag(pr, pc, kp), (((1,), (0,)), ((), ())))
            if both:
                fold(i, t, (qr - 1) * 4 + qc - 1, p, flag(qr, qc, 8 - kp), NT)

    def self_tiles(n):
        return [(1 + 2 * n + r, 1 + c, 1 + 2 * n + r, 1 + c, 8 * n + 4 * r + c) for r in range(2) for c in range(4)]

    def straight_tiles(n):
        across = [(n + 1, k, n + 1, k + 1, 15 + 6 * n + k) for k in range(1, 4)]
        return across + [(k, n + 1, k + 1, n + 1, 18 + 6 * n + k) for k in range(1, 4)]

    def diagonal_tiles(n):
        down = [(n + 1, k, n + 2, k + 1, 39 + 6 * n + k) for k in range(1, 4)]
        return down + [(n + 1, k + 1, n + 2, k, 42 + 6 * n + k) for k in range(1, 4)]

    def row_tiles(n):
        top = [(1, 1 + k, 0, n + k, 58 + 8 * n + k) for k in range(4)]
        return top + [(4, 1 + k, 5, n + k, 62 + 8 * n + k) for k in range(4)]

    def col_tiles(n):
        near = [(r, q) for r in range(1, 5) for q in range(1, 5) if abs(r - q) <= 1]
        return [(r, 1 + 3 * n, q, 5 * n, 82 + 10 * n + k) for k, (r, q) in enumerate(near)]

    def tile_loop(tiles, pick, both, count, hooks=()):
        def one(n, carry):
            for when, hook in hooks:

                @pl.when(n == when)
                def _():
                    hook()

            tiles(pick(n), both)
            return carry

        lax.fori_loop(0, count, one, 0)

    def clear(n, carry):
        dacc[n] = jnp.zeros((16, P_SIZE), F32)
        acc[n] = jnp.zeros((48, P_SIZE), F32)
        return carry

    lax.fori_loop(0, 16, clear, 0)

    own_cells(prepare)
    tile_loop(tiles_one, self_tiles, False, 2)
    tile_loop(tiles_one, diagonal_tiles, True, 3)
    if has_comm:
        expected = sum(sizes)
        for dc, ds in DIRS:
            expected = expected + inside(curve + dc, slab + ds).astype(jnp.int32)
        pl.semaphore_wait(barrier, expected)
    halo_start(kin, kin_send, kin_recv)
    min_start(0)
    tile_loop(tiles_one, straight_tiles, True, 4)
    halo_wait(kin, kin_send, kin_recv)
    halo_cells(prepare)
    tile_loop(tiles_one, row_tiles, False, 3)
    min_fold(0)
    tile_loop(tiles_one, col_tiles, False, 2, [(1, lambda: min_start(1))])

    for r in range(4):
        dens = dacc[4 * r : 4 * r + 4, 0, :] + dacc[4 * r : 4 * r + 4, 1, :]
        density_out[r] = dens
        mat = material[r]
        rest = jnp.zeros((4, P_SIZE), F32)
        base = jnp.zeros((4, P_SIZE), F32)
        grun = jnp.zeros((4, P_SIZE), F32)
        for n in range(4):
            rest = rest + jnp.where(mat == n, eos[0, n], 0.0)
            base = base + jnp.where(mat == n, eos[1, n], 0.0)
            grun = grun + jnp.where(mat == n, eos[2, n], 0.0)
        pressure = base * base * (dens - rest) + grun * dens * energy[r]
        intact = 1.0 - damage[r]
        over = 1.0 / (dens * dens)
        state[r + 1, 1:5, 0, :] = dens
        for k in range(6):
            sigma = intact * stress[k, r]
            if k < 3:
                sigma = sigma - pressure
            state[r + 1, 1:5, 2 + k, :] = sigma * over

    own_cells(prepare2)
    halo_start(state, st_send, st_recv)
    tile_loop(tiles_two, self_tiles, False, 2)
    rest = [(1, lambda: min_fold(1))]
    if len(groups) > 2:
        rest.append((2, lambda: min_start(2)))
    tile_loop(tiles_two, straight_tiles, True, 4, rest)
    tile_loop(tiles_two, diagonal_tiles, True, 3)
    halo_wait(state, st_send, st_recv)
    halo_cells(prepare2)
    tile_loop(tiles_two, row_tiles, False, 3)
    tile_loop(tiles_two, col_tiles, False, 2)
    if len(groups) > 2:
        min_fold(2)

    if has_comm:
        halo_drain(kin, kin_send, kin_recv)
        halo_drain(state, st_send, st_recv)
        for r in range(len(groups)):
            for copy in min_copies(r):
                copy.wait_send()
    step = jnp.min(msrc[len(groups) if has_comm else 0], axis=(0, 1), keepdims=True)
    step_out[...] = step

    vm = vref[...]
    for r in range(4):
        cells = slice(4 * r, 4 * r + 4)
        col_id = lax.broadcasted_iota(jnp.int32, (4, P_SIZE), 0).astype(F32)
        x = [offset[0, r] + (r + 1 - 3.0), offset[1, r] + (col_id + (1.0 - 3.0)), offset[2, r] - 0.5]
        u = [velocity[k, r] - vm[3 + k : 4 + k] for k in range(3)]
        txx, tyy, tzz, txy, txz, tyz = [state[r + 1, 1:5, 2 + k, :] for k in range(6)]
        sx = [acc[cells, k, :] for k in range(3)]
        sv = [acc[cells, 3 + k, :] for k in range(3)]
        s1 = acc[cells, 6, :]
        svx = [acc[cells, 8 + k, :] for k in range(6)]
        ax = [acc[cells, 16 + k, :] for k in range(6)]
        bx = [acc[cells, 24 + k, :] for k in range(3)]
        ux = [acc[cells, 32 + k, :] for k in range(3)]
        uv = [acc[cells, 35 + k, :] for k in range(3)]
        u1 = acc[cells, 38, :]
        uvx = acc[cells, 40, :] + acc[cells, 41, :] + acc[cells, 42, :]
        g = [x[k] * s1 - sx[k] for k in range(3)]
        push = [
            txx * g[0] + txy * g[1] + txz * g[2] + (ax[0] * x[0] + ax[3] * x[1] + ax[4] * x[2] - bx[0]),
            txy * g[0] + tyy * g[1] + tyz * g[2] + (ax[3] * x[0] + ax[1] * x[1] + ax[5] * x[2] - bx[1]),
            txz * g[0] + tyz * g[1] + tzz * g[2] + (ax[4] * x[0] + ax[5] * x[1] + ax[2] * x[2] - bx[2]),
        ]
        for k in range(3):
            drag = 0.25 * (x[k] * u1 - ux[k])
            kick_out[k, r] = step * (push[k] - drag)

        def moment(i, j):
            return u[i] * g[j] - x[j] * sv[i]

        mxx = moment(0, 0) + svx[0]
        myy = moment(1, 1) + svx[1]
        mzz = moment(2, 2) + svx[2]
        mxy = moment(0, 1) + moment(1, 0) + svx[3]
        mxz = moment(0, 2) + moment(2, 0) + svx[4]
        myz = moment(1, 2) + moment(2, 1) + svx[5]
        work = txx * mxx + tyy * myy + tzz * mzz + txy * mxy + txz * mxz + tyz * myz
        visc = uvx
        for k in range(3):
            visc = visc + u[k] * (x[k] * u1 - ux[k]) - x[k] * uv[k]
        heat_out[r] = step * (0.125 * visc - work)


def on_device(n_curve, n_slab, *args):
    vmem = pl.BlockSpec(memory_space=pltpu.VMEM)
    smem = pl.BlockSpec(memory_space=pltpu.SMEM)
    n_rounds = len(min_rounds(n_curve, n_slab))
    n_peers = max(sum(group_sizes(n_curve, n_slab)), 1)
    tiles = TILES
    square = (P_SIZE, P_SIZE)
    comm = n_curve * n_slab > 1
    params = dict(vmem_limit_bytes=56 * 1024 * 1024)
    if comm:
        params.update(collective_id=0, has_side_effects=True)
    density, kick, heat, step = pl.pallas_call(
        functools.partial(body, n_curve, n_slab),
        out_shape=(
            jax.ShapeDtypeStruct((4, 4, P_SIZE), F32),
            jax.ShapeDtypeStruct((3, 4, 4, P_SIZE), F32),
            jax.ShapeDtypeStruct((4, 4, P_SIZE), F32),
            jax.ShapeDtypeStruct((1, 1), F32),
        ),
        in_specs=[vmem] * 8 + [smem, smem],
        out_specs=(vmem, vmem, vmem, vmem),
        scratch_shapes=[
            pltpu.VMEM((6, 6, 8, P_SIZE), F32),
            pltpu.VMEM((6, 6, 8, P_SIZE), F32),
            pltpu.VMEM((36, P_SIZE, 64), BF16),
            pltpu.VMEM((36, 64, 3 * P_SIZE), BF16),
            pltpu.VMEM((36, P_SIZE, 32), BF16),
            pltpu.VMEM((36, 32, 2 * P_SIZE), BF16),
            pltpu.VMEM((36, 32, P_SIZE), BF16),
            pltpu.VMEM((8, P_SIZE), F32),
            pltpu.VMEM((36, 64, P_SIZE), BF16),
            pltpu.VMEM((36, 32, P_SIZE), BF16),
            [pltpu.VMEM((P_SIZE, 3 * P_SIZE), F32) for _ in range(WIDEST)],
            [pltpu.VMEM(square, BF16) for _ in range(WIDEST)],
            [pltpu.VMEM(square, BF16) for _ in range(WIDEST)],
            pltpu.VMEM((tiles, *square), BF16),
            pltpu.VMEM((tiles, *square), BF16),
            pltpu.VMEM((tiles, *square), F32),
            pltpu.VMEM((tiles, *square), F32),
            pltpu.VMEM((16, 16, P_SIZE), F32),
            pltpu.VMEM((16, 48, P_SIZE), F32),
            pltpu.VMEM((8, P_SIZE), F32),
            pltpu.VMEM((n_rounds + 1, 8, P_SIZE), F32),
            pltpu.VMEM((n_peers, 8, P_SIZE), F32),
            pltpu.SemaphoreType.DMA((8,)),
            pltpu.SemaphoreType.DMA((8,)),
            pltpu.SemaphoreType.DMA((8,)),
            pltpu.SemaphoreType.DMA((8,)),
            pltpu.SemaphoreType.DMA((n_peers,)),
            pltpu.SemaphoreType.DMA((n_peers,)),
        ],
        compiler_params=pltpu.CompilerParams(**params),
    )(*args)
    return density, kick, heat, step[0, 0]


def solution(mesh):
    in_specs = (
        P(None, "curve", "slab", None),
        P(None, "curve", "slab", None),
        P("curve", "slab", None),
        P("curve", "slab", None),
        P("curve", "slab", None),
        P("curve", "slab", None),
        P(None, "curve", "slab", None),
        P("curve", "slab", None),
        P("curve", "slab", None),
        P(),
    )
    out_specs = (
        P("curve", "slab", None),
        P(None, "curve", "slab", None),
        P("curve", "slab", None),
        P(),
    )
    run = functools.partial(on_device, mesh.shape["curve"], mesh.shape["slab"])
    return jax.shard_map(run, mesh=mesh, in_specs=in_specs, out_specs=out_specs, check_vma=False)
```
